32 devices in a mesh: tm: 8 (over y, x, core), cuts: 4 (over z).
Axes of the slice: x: 2, y: 2, z: 4, core: 2. Of those that a mesh axis runs over, the one named last changes fastest.
Arguments:
- volume: float32 [16, 32, 24, 1024], P('tm', 'cuts'), may hold values from -6 to 6
- measured: bfloat16 [16, 6, 32, 24, 1024], P('tm', None, 'cuts'), may hold values from -6 to 6
- counts: int32 [16], P('tm'), may hold values from 2 to 6, as said below
- vshift: int32 [16, 6], P('tm'), may hold values from -2 to 2, as said below
- hshift: int32 [16, 6], P('tm'), may hold values from -16 to 16
- angles: int32 [16, 6], P('tm'), may hold values from 0 to 3
- blocks: bfloat16 [4, 1024, 1024], replicated, may hold values from -0.1875 to 0.1875
Outputs:
- gradient: float32 [16, 32, 24, 1024], P('tm', 'cuts')
The draws below stay inside these ranges and needn't reach their ends.
Inputs may be any that keep to these rules, and one draw needn't show every extreme that they name: `counts`: some frame has exactly 2 live views and another exactly 6. `vshift`: some live view has the shift 2 and another -2.
All inputs are finite; a program needn't handle non-finite values.
Results may differ from the reference program's by a relative error of at most 0.0029.
Values may be sent and summed in bfloat16 or wider, within the bound.
A program may use at most 64 MiB of HBM per device.

```python
from functools import partial
import jax
import jax.numpy as jnp
from jax import lax

Y = 1024
DET = 1024
XW = 24
VCAP = 6
NA = 4
H = 2
SH = 16
F = 16
Z = 32


def draw_counts(key, part):
    values = jax.random.randint(key, (F,), 2, VCAP + 1)
    picked = jax.random.fold_in(key, 21)
    frame_low = jax.random.randint(jax.random.fold_in(picked, 1), (), 0, F)
    frame_high = (frame_low + 1 + jax.random.randint(jax.random.fold_in(picked, 2), (), 0, F - 1)) % F
    values = values.at[frame_low].set(2).at[frame_high].set(VCAP)
    return values.astype(jnp.int32)


def draw_vshift(key, part):
    values = jax.random.randint(key, (F, VCAP), -H, H + 1)
    picked = jax.random.fold_in(key, 37)
    frame_low = jax.random.randint(jax.random.fold_in(picked, 1), (), 0, F)
    frame_high = jax.random.randint(jax.random.fold_in(picked, 2), (), 0, F)
    view_low = jax.random.randint(jax.random.fold_in(picked, 3), (), 0, 1)
    view_high = 1 - view_low
    values = values.at[frame_low, view_low].set(-H).at[frame_high, view_high].set(H)
    return values.astype(jnp.int32)


def place_ends(array, key, least, top_value):
    dims = array.shape
    index_at = [jax.random.randint(jax.random.fold_in(key, axis), (), 0, dims[axis]) for axis in range(len(dims))]
    array = array.at[tuple(index_at)].set(least)
    longest = dims.index(max(dims))
    index_at[longest] = (index_at[longest] + 1) % dims[longest]
    return array.at[tuple(index_at)].set(top_value)


def level_of(rng, dims, cuts, least, high):
    gain, own = 1.0, jax.random.fold_in(rng, 6)
    for dim, shards_of in cuts:
        steps = jnp.exp(jax.random.uniform(jax.random.fold_in(own, dim), (shards_of,), jnp.float32, least / len(cuts), high / len(cuts)))
        gain = gain * jnp.repeat(steps, dims[dim] // shards_of).reshape([-1 if axis == dim else 1 for axis in range(len(dims))])
    return gain


def scatter_about(stream_key, dims, width, reach, shards=(), held_as=jnp.bfloat16):
    drawn = jax.random.normal(stream_key, dims, jnp.float32) * width
    if len(shards) > 0:
        drawn = level_of(stream_key, dims, shards, -0.22, 0.18) * drawn
    return jnp.clip(drawn, min=-reach, max=reach).astype(held_as)


def setup_inputs(seed: int = 0) -> dict:
    arg_keys = jax.random.split(jax.random.key(seed), 8)
    volume = scatter_about(arg_keys[0], (F, Z, XW, Y), 1.0, 6.0, ((0, 8), (1, 4)), jnp.float32)
    measured = scatter_about(arg_keys[1], (F, VCAP, Z, XW, DET), 1.0, 6.0, ((0, 8), (2, 4)))
    counts = draw_counts(jax.random.fold_in(arg_keys[7], 71), 0)
    vshift = draw_vshift(jax.random.fold_in(arg_keys[7], 71), 0)
    hshift = place_ends(jax.random.randint(arg_keys[4], (F, VCAP), -SH, SH + 1), jax.random.fold_in(arg_keys[4], 1), -SH, SH).astype(jnp.int32)
    angles = place_ends(jax.random.randint(arg_keys[5], (F, VCAP), 0, NA), jax.random.fold_in(arg_keys[5], 1), 0, NA - 1).astype(jnp.int32)
    blocks = scatter_about(arg_keys[6], (NA, Y, DET), Y ** -0.5, 0.1875)
    return {"volume": volume, "measured": measured, "counts": counts, "vshift": vshift, "hshift": hshift, "angles": angles, "blocks": blocks}


def shift_cols(values, amount):
    padded = jnp.pad(values, [(0, 0)] * (values.ndim - 1) + [(SH, SH)])
    return lax.dynamic_slice_in_dim(padded, SH - amount, values.shape[-1], values.ndim - 1)

def view_residual(extended, measured_frame, vertical, lateral, angle_ids, blocks, count, masked, view_no, totals):
    slices = measured_frame.shape[1]
    block = lax.dynamic_index_in_dim(blocks, angle_ids[view_no], 0, keepdims=False)
    offset = H + vertical[view_no]
    lateral_now = lateral[view_no]
    source_frame = lax.dynamic_slice_in_dim(extended, offset, slices, 0)
    image = jnp.dot(source_frame.reshape(-1, source_frame.shape[-1]), block, preferred_element_type=jnp.float32)
    image = image.reshape(measured_frame.shape[1:])
    seen = lax.dynamic_index_in_dim(measured_frame, view_no, 0, keepdims=False)
    misfit = shift_cols(image, lateral_now) - seen.astype(jnp.float32)
    if masked:
        misfit = misfit * (view_no < count).astype(jnp.float32)
    spread = shift_cols(misfit.astype(jnp.bfloat16), -lateral_now)
    back = lax.dot_general(spread.reshape(-1, spread.shape[-1]), block, (((1,), (1,)), ((), ())), preferred_element_type=jnp.float32)
    back = back.reshape(source_frame.shape)
    present_frame = lax.dynamic_slice_in_dim(totals, offset, slices, 0)
    return lax.dynamic_update_slice_in_dim(totals, present_frame + back, offset, 0)

def reference(volume, measured, counts, vshift, hshift, angles, blocks):
    lowered = volume.astype(jnp.bfloat16)
    extended = jnp.pad(lowered, ((0, 0), (H, H), (0, 0), (0, 0)))

    def frame_fit(frame_number):
        extended_frame_index = lax.dynamic_index_in_dim(extended, frame_number, 0, keepdims=False)
        measurement_frame = lax.dynamic_index_in_dim(measured, frame_number, 0, keepdims=False)
        step_forward = partial(view_residual, extended_frame_index, measurement_frame, vshift[frame_number], hshift[frame_number], angles[frame_number], blocks, counts[frame_number], True)
        totals = lax.fori_loop(0, VCAP, step_forward, jnp.zeros(extended_frame_index.shape, jnp.float32))
        return totals[H:H + Z]
    fitted_volume = lax.map(frame_fit, jnp.arange(F, dtype=jnp.int32))
    differ = volume[1:] - volume[:-1]
    weight = differ / jnp.sqrt(differ * differ + 0.25)
    varied = jnp.pad(weight, ((1, 0), (0, 0), (0, 0), (0, 0))) - jnp.pad(weight, ((0, 1), (0, 0), (0, 0), (0, 0)))
    return fitted_volume + 0.5 * varied
```

```python
from functools import partial

import jax
import jax.numpy as jnp
from jax import lax
from jax.experimental import pallas as pl
from jax.experimental.pallas import tpu as pltpu
from jax.sharding import PartitionSpec as P

H = 2
LANES = 128
NT = (((1,), (1,)), ((), ()))
MESH = pl.DeviceIdType.MESH


def lateral(x, by):
    columns = x.shape[1] // LANES
    lane = lax.broadcasted_iota(jnp.int32, (x.shape[0], LANES), 1)
    take_next, take_last = lane >= LANES - by, lane < -by
    amount = lax.rem(LANES - by, LANES)
    zero = jnp.zeros((x.shape[0], LANES), x.dtype)
    turned = [pltpu.roll(x[:, c * LANES : (c + 1) * LANES], amount, 1) for c in range(columns)]
    turned = [zero] + turned + [zero]
    return [
        jnp.where(take_next, turned[c + 2], jnp.where(take_last, turned[c], turned[c + 1]))
        for c in range(columns)
    ]


def ordered(count, kind_of, kinds, views):
    keys = [jnp.where(v < count, kind_of[v], kinds) for v in range(views)]
    ranks = []
    for v in range(views):
        rank = jnp.int32(0)
        for u in range(views):
            if u != v:
                ahead = keys[u] <= keys[v] if u < v else keys[u] < keys[v]
                rank = rank + jnp.where(ahead, 1, 0)
        ranks.append(rank)
    view_at, key_at = [], []
    for j in range(views):
        view, key = jnp.int32(0), jnp.int32(0)
        for v in range(views):
            view = view + jnp.where(ranks[v] == j, v, 0)
            key = key + jnp.where(ranks[v] == j, keys[v], 0)
        view_at.append(view)
        key_at.append(key)
    return view_at, key_at


def kernel(
    seen_count, counts, vshift, hshift, angles, volume_in, measured_in, blocks_in, out, *scratch
):
    seen = scratch[:seen_count]
    compute(
        seen, counts, vshift, hshift, angles, volume_in, measured_in, blocks_in, out, *scratch[seen_count:]
    )


def compute(
    seen, counts, vshift, hshift, angles, volume_in, measured_in, blocks_in, out,
    volume, blocks, low, sums, ways, image, terms, rim_rows, rim_fit,
    up, down, below, above, before, after, load_sem, block_sem, send_sem, recv_sem,
):
    frames, views, slices, height, width = measured_in.shape
    kinds = blocks_in.shape[0]
    rows, rim = slices * height, H * height
    wide = slices + 2 * H
    slab, cuts = lax.axis_index("cuts"), lax.axis_size("cuts")
    time, times = lax.axis_index("tm"), lax.axis_size("tm")
    has_below, has_above = slab > 0, slab + 1 < cuts
    has_before, has_after = time > 0, time + 1 < times
    next_slab, last_slab = lax.rem(slab + 1, cuts), lax.rem(slab + cuts - 1, cuts)
    next_time, last_time = lax.rem(time + 1, times), lax.rem(time + times - 1, times)

    get_volume = pltpu.make_async_copy(volume_in, volume, load_sem.at[0])
    get_volume.start()

    def get_block(a):
        return pltpu.make_async_copy(blocks_in.at[a], blocks.at[a], block_sem.at[a])

    get_block(0).start()
    blank = jnp.zeros((2 * H, height, width), seen[0].dtype)
    get_seen = []
    for f in range(frames):
        for v in range(views):
            seen[f][v, : 2 * H] = blank
            seen[f][v, 2 * H + slices :] = blank
        get_seen.append(
            pltpu.make_async_copy(
                measured_in.at[f], seen[f].at[:, pl.ds(2 * H, slices)], load_sem.at[1 + f]
            )
        )
        get_seen[f].start()
        if f + 1 < kinds:
            get_block(f + 1).start()
    for a in range(frames + 1, kinds):
        get_block(a).start()
    barrier = pltpu.get_barrier_semaphore()
    neighbours = (
        (has_below, {"cuts": last_slab}),
        (has_above, {"cuts": next_slab}),
        (has_before, {"tm": last_time}),
        (has_after, {"tm": next_time}),
    )
    for there, device in neighbours:

        @pl.when(there)
        def _():
            pl.semaphore_signal(barrier, inc=1, device_id=device, device_id_type=MESH)

    for f in range(frames):
        sums[views, f] = jnp.zeros(sums.shape[2:], sums.dtype)
        ways[views, f] = jnp.zeros(ways.shape[2:], ways.dtype)
    for there, ref in ((has_below, below), (has_above, above), (has_before, before), (has_after, after)):

        @pl.when(jnp.logical_not(there))
        def _():
            ref[...] = jnp.zeros(ref.shape, ref.dtype)

    get_volume.wait()
    for f in range(frames):
        low[f * rows : (f + 1) * rows] = volume[f].astype(low.dtype)

    pl.semaphore_wait(barrier, sum(jnp.where(there, 1, 0) for there, _ in neighbours))

    def remote(src, dst, n, device):
        return pltpu.make_async_remote_copy(
            src_ref=src,
            dst_ref=dst,
            send_sem=send_sem.at[n],
            recv_sem=recv_sem.at[n],
            device_id=device,
            device_id_type=MESH,
        )

    transfers = (
        (remote(low.at[pl.ds((frames - 1) * rows, rows)], before, 0, {"tm": next_time}), has_after, has_before),
        (remote(low.at[pl.ds(0, rows)], after, 1, {"tm": last_time}), has_before, has_after),
        (remote(up, below, 2, {"cuts": next_slab}), has_above, has_below),
        (remote(down, above, 3, {"cuts": last_slab}), has_below, has_above),
    )

    def begin(transfer):
        copy, sends, _ = transfer

        @pl.when(sends)
        def _():
            copy.start()

    begin(transfers[0])
    begin(transfers[1])
    share = kinds // frames
    part = wide // share

    for f in range(frames):
        view_at, key_at = ordered(
            counts[f], [angles[f, v] for v in range(views)], kinds, views
        )
        vertical, side = [vshift[f, v] for v in view_at], [hshift[f, v] for v in view_at]
        same = [
            jnp.where(key_at[j] == key_at[j - 1], 1, 0).astype(jnp.float32) for j in range(1, views)
        ]
        for j in range(views):
            z = lax.broadcasted_iota(jnp.int32, (slices, width), 0) + (slab * slices - vertical[j])
            e = lax.broadcasted_iota(jnp.int32, (slices, width), 1) + side[j]
            inside = (z >= 0) & (z < cuts * slices) & (e >= 0) & (e < width)
            inside = jnp.where(inside, 1.0, 0.0)
            ways[j, f] = inside if j == 0 else inside + same[j - 1] * ways[j - 1, f]
        get_seen[f].wait()

        def add_slice(z):
            for j in range(views):
                x = seen[f][view_at[j], z + H - vertical[j]].astype(jnp.float32)
                for c, y in enumerate(lateral(x, side[j])):
                    lanes = pl.ds(c * LANES, LANES)
                    if j > 0:
                        y = y + same[j - 1] * sums[j - 1, f, z, :, lanes]
                    sums[j, f, z, :, lanes] = y

        def project(k, carry):
            a = f * share + k
            get_block(a).wait()
            for q in range(2):
                lanes = pl.ds(q * width // 2, width // 2)
                image[a, :, lanes] = jnp.dot(
                    low[...], blocks[a, :, lanes], preferred_element_type=jnp.float32
                )
                for i in range(q * part // 2, (q + 1) * part // 2):
                    add_slice(k * part + i)
            return carry

        lax.fori_loop(0, share, project, 0)

    def slot_of(f, a):
        upto, here = jnp.int32(0), jnp.int32(0)
        for v in range(views):
            live = v < counts[f]
            upto = upto + jnp.where(jnp.logical_and(live, angles[f, v] <= a), 1, 0)
            here = here + jnp.where(jnp.logical_and(live, angles[f, v] == a), 1, 0)
        return jnp.where(here > 0, upto - 1, views)

    def rims(a, carry):
        for f in range(frames):
            slot = slot_of(f, a)
            for i in range(H):
                at = f * rim + i * height
                rim_rows[at : at + height] = sums[slot, f, H + slices + i].astype(rim_rows.dtype)
                at += frames * rim
                rim_rows[at : at + height] = sums[slot, f, i].astype(rim_rows.dtype)
        rim_fit[...] += lax.dot_general(rim_rows[...], blocks[a], NT, preferred_element_type=jnp.float32)
        return carry

    rim_fit[...] = jnp.zeros_like(rim_fit)
    lax.fori_loop(0, kinds, rims, 0)
    for f in range(frames):
        up[f] = rim_fit[f * rim : (f + 1) * rim].astype(up.dtype)
        down[f] = rim_fit[(frames + f) * rim : (frames + f + 1) * rim].astype(down.dtype)
        out[f] = jnp.zeros(out.shape[1:], out.dtype)
    begin(transfers[2])
    begin(transfers[3])

    def end(transfer):
        copy, sends, takes = transfer

        @pl.when(sends)
        def _():
            copy.wait_send()

        @pl.when(takes)
        def _():
            copy.wait_recv()

    end(transfers[0])
    end(transfers[1])
    first_factor = jnp.where(has_before, 0.5, 0.0).astype(jnp.float32)
    last_factor = jnp.where(has_after, 0.5, 0.0).astype(jnp.float32)
    stripe = rows // kinds

    def smooth(a):
        part = pl.ds(pl.multiple_of(a * stripe, stripe), stripe)
        held = [before[part].astype(jnp.float32)] + [volume[f, part] for f in range(frames)]
        held += [after[part].astype(jnp.float32)]
        weights = []
        for f in range(frames + 1):
            differ = held[f + 1] - held[f]
            weights.append(differ * lax.rsqrt(differ * differ + 0.25))
        for f in range(frames):
            ahead = first_factor if f == 0 else 0.5
            behind = last_factor if f == frames - 1 else 0.5
            out[f, part] += ahead * weights[f] - behind * weights[f + 1]

    def main(a, carry):
        for f in range(frames):
            slot = slot_of(f, a)
            for z in range(slices):
                at = f * rows + z * height
                way = ways[slot, f, z : z + 1, :]
                term = way * image[a, at : at + height] - sums[slot, f, H + z]
                terms[at : at + height] = term.astype(terms.dtype)
        back = lax.dot_general(terms[...], blocks[a], NT, preferred_element_type=jnp.float32)
        for f in range(frames):
            out[f] += back[f * rows : (f + 1) * rows]

        smooth(a)
        return carry

    lax.fori_loop(0, kinds, main, 0)

    end(transfers[2])
    end(transfers[3])
    for f in range(frames):
        out[f, :rim] -= below[f].astype(jnp.float32)
        out[f, rows - rim :] -= above[f].astype(jnp.float32)


def body(volume, measured, counts, vshift, hshift, angles, blocks):
    frames, slices, height, width = volume.shape
    views, kinds = measured.shape[1], blocks.shape[0]
    rows, rim = slices * height, H * height
    smem = pl.BlockSpec(memory_space=pltpu.SMEM)
    anywhere = pl.BlockSpec(memory_space=pl.ANY)
    low_type, wide_type = jnp.bfloat16, jnp.float32
    out = pl.pallas_call(
        partial(kernel, frames),
        in_specs=[smem] * 4 + [anywhere] * 3,
        out_specs=pl.BlockSpec(memory_space=pltpu.VMEM),
        out_shape=pltpu.VMEM((frames, rows, width), wide_type),
        scratch_shapes=[pltpu.VMEM((views, slices + 4 * H, height, width), low_type)] * frames
        + [
            pltpu.VMEM((frames, rows, width), wide_type),
            pltpu.VMEM((kinds, width, width), low_type),
            pltpu.VMEM((frames * rows, width), low_type),
            pltpu.VMEM((views + 1, frames, slices + 2 * H, height, width), wide_type),
            pltpu.VMEM((views + 1, frames, slices, width), wide_type),
            pltpu.VMEM((kinds, frames * rows, width), wide_type),
            pltpu.VMEM((frames * rows, width), low_type),
            pltpu.VMEM((2 * frames * rim, width), low_type),
            pltpu.VMEM((2 * frames * rim, width), wide_type),
        ]
        + [pltpu.VMEM((frames, rim, width), low_type)] * 4
        + [pltpu.VMEM((rows, width), low_type)] * 2
        + [
            pltpu.SemaphoreType.DMA((1 + frames,)),
            pltpu.SemaphoreType.DMA((kinds,)),
            pltpu.SemaphoreType.DMA((4,)),
            pltpu.SemaphoreType.DMA((4,)),
        ],
        compiler_params=pltpu.CompilerParams(
            collective_id=0, has_side_effects=True, vmem_limit_bytes=61 * 2**20
        ),
        name="gradient",
    )(
        counts,
        vshift,
        hshift,
        angles,
        volume.reshape(frames, rows, width),
        measured,
        blocks,
    )
    return out.reshape(frames, slices, height, width)


def solution(mesh):
    in_specs = (
        P("tm", "cuts", None, None),
        P("tm", None, "cuts", None, None),
        P("tm"),
        P("tm", None),
        P("tm", None),
        P("tm", None),
        P(),
    )
    out_specs = P("tm", "cuts", None, None)
    return jax.shard_map(body, mesh=mesh, in_specs=in_specs, out_specs=out_specs, check_vma=False)
```
